512 devices in a mesh: frames: 64 (over x, y, core), cols: 8 (over z).
Axes of the slice: x: 4, y: 8, z: 8, core: 2. Of those that a mesh axis runs over, the one named last changes fastest.
Arguments:
- panel: float32 [32768, 512], P('frames', 'cols'), may hold values from -12 to 12
- trailing: float32 [32768, 4096], P('frames', 'cols'), may hold values from -6 to 6
Outputs:
- r_factor: float32 [512, 512], P('frames')
- coupling: float32 [512, 4096], P('frames', 'cols')
- remainder: float32 [32768, 4096], P('frames', 'cols')
The draws below stay inside these ranges and needn't reach their ends.
All inputs are finite; a program needn't handle non-finite values.
Results may differ from the reference program's by a relative error of at most 0.0003.
Values sent between devices are 32-bit elements; how exact they have to be, the bound alone decides.
A program may use at most 64 MiB of HBM per device.

```python
import jax
import jax.numpy as jnp
from jax import lax

PANEL = 512
TRAIL = 4096
ROWS = 32768


def draw_panel(key, part):
    first = jax.random.fold_in(key, 0)
    row_pos = jnp.arange(ROWS)[:, None] % PANEL
    col_pos = jnp.arange(PANEL)[None, :]
    eye_part = jnp.where(row_pos == col_pos, 2.0, 0.0).astype(jnp.float32)
    noise = jax.random.normal(first, (ROWS, PANEL), jnp.float32)
    return eye_part + 0.6 * noise / jnp.sqrt(1.0 * PANEL)


def steps_of(key, dims, pieces, low, high):
    gain, own = 1.0, jax.random.fold_in(key, 6)
    for position, shards_of in pieces:
        heights = jnp.exp(jax.random.uniform(jax.random.fold_in(own, position), (shards_of,), jnp.float32, low / len(pieces), high / len(pieces)))
        gain = gain * jnp.repeat(heights, dims[position] // shards_of).reshape([-1 if axis == position else 1 for axis in range(len(dims))])
    return gain


def gaussian(rng, shape, spread, reach, pieces=(), kind=jnp.bfloat16):
    level = steps_of(rng, shape, pieces, -0.22, 0.18) if pieces else 1.0
    entries = jax.random.normal(rng, shape, jnp.float32) * spread * level
    return jnp.minimum(jnp.maximum(entries, -reach), reach).astype(kind)


def setup_inputs(seed: int = 0) -> dict:
    seeds = jax.random.split(jax.random.key(seed), 3)
    panel = draw_panel(jax.random.fold_in(seeds[2], 71), 0)
    trailing = gaussian(seeds[1], (ROWS, TRAIL), 1.0, 6.0, ((0, 64), (1, 8)), jnp.float32)
    return dict(panel=panel, trailing=trailing)


def reference(panel, trailing):
    upper = jnp.linalg.qr(panel, mode='r')
    signs = jnp.sign(jnp.diagonal(upper))
    upper = upper * signs[:, None]
    cross = jnp.dot(panel.T, trailing, precision=lax.Precision.HIGHEST)
    coupling = jax.scipy.linalg.solve_triangular(upper.T, cross, lower=True)
    weights = jax.scipy.linalg.solve_triangular(upper, coupling, lower=False)
    remainder = trailing - jnp.dot(panel, weights, precision=lax.Precision.HIGHEST)
    return (upper, coupling, remainder)
```

```python
import functools

import jax
import jax.numpy as jnp
from jax import lax
from jax.experimental import pallas as pl
from jax.experimental.pallas import tpu as pltpu
from jax.sharding import PartitionSpec as P

HI = lax.Precision.HIGHEST
F32 = jnp.float32
MESH = pl.DeviceIdType.MESH


def frame_dims(frames):
    return {64: (4, 8, 2), 8: (2, 2, 2)}[frames]


def sum_slots(ref):
    total = ref[0]
    for slot in range(1, ref.shape[0]):
        total = total + ref[slot]
    return total


def reduce_kernel(
    dims, panel_ref, trail_ref, rt_ref, g_ref, c_ref,
    gp, gcore, gs, gx, gy, xs, xo, xcore, xx, xr, xy,
    ring_send, ring_recv, core_send, core_recv, x_send, x_recv, y_send, y_recv, z_send, z_recv,
):
    nx, ny, nq, nz = dims
    f = lax.axis_index("frames")
    z = lax.axis_index("cols")
    q = lax.rem(f, nq)
    y = lax.rem(f // nq, ny)
    x = f // (nq * ny)

    def device(x=x, y=y, q=q, z=z):
        return ((x * ny + y) * nq + q, z)

    def step(me, d, n):
        return lax.rem(me + d, n)

    partners = [device(q=step(q, d, nq)) for d in range(1, nq)]
    partners += [device(x=step(x, d, nx)) for d in range(1, nx)]
    partners += [device(y=step(y, d, ny)) for d in range(1, ny)]
    partners += [device(z=step(z, d, nz)) for d in range(1, nz)]
    barrier = pltpu.get_barrier_semaphore()
    for other in partners:
        pl.semaphore_signal(barrier, inc=1, device_id=other, device_id_type=MESH)
    width = panel_ref.shape[1]
    rt_ref[pl.ds(pl.multiple_of(z * width, width), width), :] = panel_ref[...].T
    pl.semaphore_wait(barrier, len(partners))

    pending = []

    def push(src, dst, send, recv, to):
        copy = pltpu.make_async_remote_copy(
            src_ref=src, dst_ref=dst, send_sem=send, recv_sem=recv, device_id=to, device_id_type=MESH
        )
        copy.start()
        pending.append(copy)
        return copy

    def arrived(copies):
        for copy in copies:
            copy.wait_recv()

    half = width // 2
    last = nz // 2 - 1
    moving = {}
    for s in range(nz // 2):
        for piece in range(2):
            for way in range(2):
                if s == last and piece != way:
                    continue
                if s > 0:
                    moving[s - 1, piece, way].wait_recv()
                owner = lax.rem(z + nz - s, nz) if way == 0 else lax.rem(z + s, nz)
                there = step(z, 1, nz) if way == 0 else step(z, nz - 1, nz)
                block = rt_ref.at[pl.ds(pl.multiple_of(owner * width + piece * half, half), half), :]
                moving[s, piece, way] = push(
                    block, block, ring_send.at[way, s, piece], ring_recv.at[way, s, piece], device(z=there)
                )
    waited = {key for key in moving if (key[0] + 1, key[1], key[2]) in moving}
    for key in moving:
        if key not in waited:
            moving[key].wait_recv()

    own = rt_ref[pl.ds(pl.multiple_of(z * width, width), width), :]
    gp[...] = lax.dot_general(
        own, rt_ref[...], (((1,), (1,)), ((), ())), precision=HI, preferred_element_type=F32
    ).reshape(gp.shape)
    other_q = step(q, 1, nq)
    core = device(q=other_q)
    g_core = [push(gp.at[other_q], gcore, core_send.at[0], core_recv.at[0], core)]

    rows = rt_ref.shape[0] // nq

    def cross(part):
        left = rt_ref[pl.ds(pl.multiple_of(part * rows, rows), rows), :]
        return jnp.dot(left, trail_ref[...], precision=HI, preferred_element_type=F32).reshape(xs.shape)

    xs[...] = cross(other_q)
    x_core = [push(xs, xcore, core_send.at[1], core_recv.at[1], core)]
    xo[...] = cross(q)

    arrived(g_core)
    gs[...] = gp[q] + gcore[...]
    gx[x] = gs[x]

    def along_x(stage, src, dst):
        return [
            push(src(step(x, d, nx)), dst, x_send.at[stage, d], x_recv.at[stage, d], device(x=step(x, d, nx)))
            for d in range(1, nx)
        ]

    def along_y(stage, src, dst):
        return [
            push(src(step(y, d, ny)), dst, y_send.at[stage, d], y_recv.at[stage, d], device(y=step(y, d, ny)))
            for d in range(1, ny)
        ]

    g_x = along_x(0, lambda to: gs.at[to], gx.at[x])
    arrived(x_core)
    xo[...] = xo[...] + xcore[...]
    xx[x] = xo[x]
    x_x = along_x(1, lambda to: xo.at[to], xx.at[x])
    arrived(g_x)
    gy[y] = sum_slots(gx)
    g_y = along_y(0, lambda to: gy.at[y], gy.at[y])
    arrived(x_x)
    xr[...] = sum_slots(xx)
    xy[y] = xr[y]
    x_y = along_y(1, lambda to: xr.at[to], xy.at[y])
    arrived(g_y)
    g_ref[z, q, x] = sum_slots(gy)
    piece = g_ref.at[z, q, x]
    g_z = [
        push(piece, piece, z_send.at[d], z_recv.at[d], device(z=step(z, d, nz))) for d in range(1, nz)
    ]
    arrived(x_y)
    c_ref[q, x, y] = sum_slots(xy)
    x_y = along_y(2, lambda to: c_ref.at[q, x, y], c_ref.at[q, x, y])
    arrived(g_z)
    g_x = along_x(2, lambda to: g_ref.at[:, q, x], g_ref.at[:, q, x])
    arrived(x_y)
    x_x = along_x(3, lambda to: c_ref.at[q, x], c_ref.at[q, x])
    arrived(g_x)
    g_core = [push(g_ref.at[:, q], g_ref.at[:, q], core_send.at[2], core_recv.at[2], core)]
    arrived(x_x)
    x_core = [push(c_ref.at[q], c_ref.at[q], core_send.at[3], core_recv.at[3], core)]
    arrived(g_core)
    arrived(x_core)
    for copy in pending:
        copy.wait_send()


def reduce_products(dims, panel, trail):
    nx, ny, nq, nz = dims
    height, width = panel.shape
    cols = trail.shape[1]
    n = width * nz
    rg = n // (nz * nq * nx)
    rx = n // (nq * nx * ny)
    vm = pl.BlockSpec(memory_space=pltpu.VMEM)
    dma = pltpu.SemaphoreType.DMA
    rt, g, c = pl.pallas_call(
        functools.partial(reduce_kernel, dims),
        out_shape=(
            jax.ShapeDtypeStruct((n, height), F32),
            jax.ShapeDtypeStruct((nz, nq, nx, rg, n), F32),
            jax.ShapeDtypeStruct((nq, nx, ny, rx, cols), F32),
        ),
        in_specs=[vm, vm],
        out_specs=(vm,) * 3,
        scratch_shapes=[
            pltpu.VMEM((nq, nx, rg, n), F32),
            pltpu.VMEM((nx, rg, n), F32),
            pltpu.VMEM((nx, rg, n), F32),
            pltpu.VMEM((nx, rg, n), F32),
            pltpu.VMEM((ny, rg, n), F32),
            pltpu.VMEM((nx, ny, rx, cols), F32),
            pltpu.VMEM((nx, ny, rx, cols), F32),
            pltpu.VMEM((nx, ny, rx, cols), F32),
            pltpu.VMEM((nx, ny, rx, cols), F32),
            pltpu.VMEM((ny, rx, cols), F32),
            pltpu.VMEM((ny, rx, cols), F32),
            dma((2, nz // 2, 2)), dma((2, nz // 2, 2)),
            dma((4,)), dma((4,)),
            dma((4, nx)), dma((4, nx)),
            dma((3, ny)), dma((3, ny)),
            dma((nz,)), dma((nz,)),
        ],
        compiler_params=pltpu.CompilerParams(
            collective_id=0, has_side_effects=True, vmem_limit_bytes=40 * 2**20
        ),
        name="reduce_products",
    )(panel, trail)
    return rt, g.reshape(n, n), c.reshape(n, cols)


def split3(v):
    h = v.astype(jnp.bfloat16).astype(F32)
    rest = v - h
    m = rest.astype(jnp.bfloat16).astype(F32)
    low = rest - m
    return h, m, low

def lane(v, c):
    return jnp.broadcast_to(v[:, c:c + 1], v.shape)

def factor_block(s_ref, m_ref):
    n = s_ref.shape[0]
    steps = n // 8
    sub = lax.broadcasted_iota(jnp.int32, (8, n), 0)
    col = lax.broadcasted_iota(jnp.int32, (8, n), 1)
    x = [jnp.broadcast_to(s_ref[i:i + 1, :], (8, n)) for i in range(8)]
    d = [[lane(x[i], k) for k in range(i + 1)] for i in range(8)]
    for j in range(steps):
        base = 8 * j
        own = (col >= base) & (col < base + 8)
        x = [jnp.where(own, jnp.where(col == base + i, 1.0, 0.0), x[i]) for i in range(8)]
        u = []
        low = [[None] * 8 for _ in range(8)]
        for k in range(8):
            scale = lax.rsqrt(d[k][k])
            for i in range(k + 1, 8):
                low[i][k] = d[i][k] * scale
            for i in range(k + 1, 8):
                for m in range(k + 1, i + 1):
                    d[i][m] = d[i][m] - low[i][k] * low[m][k]
            u.append(x[k] * scale)
            for i in range(k + 1, 8):
                x[i] = x[i] - low[i][k] * u[k]
        packed = u[7]
        for k in range(7):
            packed = jnp.where(sub == k, u[k], packed)
        m_ref[base:base + 8, :] = jnp.where(col < base + 8, packed, 0.0)
        if j == steps - 1:
            break
        nxt = base + 8
        if j + 2 < steps:
            h, mid, lo = split3(packed)
            left = jnp.concatenate([h, h, mid, mid, h, lo], axis=0).astype(jnp.bfloat16)
            right = jnp.concatenate([h, mid, h, mid, lo, h], axis=0).astype(jnp.bfloat16)
            update = lax.dot_general(left, right, (((0,), (0,)), ((), ())), preferred_element_type=F32)
        x = [jnp.broadcast_to(s_ref[nxt + i:nxt + i + 1, :], (8, n)) for i in range(8)]
        d = [[lane(x[i], nxt + k) for k in range(i + 1)] for i in range(8)]
        x = [jnp.where(own, 0.0, v) for v in x]
        for k in range(8):
            w = [lane(u[k], nxt + i) for i in range(8)]
            for i in range(8):
                x[i] = x[i] - w[i] * u[k]
                for m in range(i + 1):
                    d[i][m] = d[i][m] - w[i] * w[m]
        if j + 2 < steps:
            for p in range(j + 2, steps):
                s_ref[8 * p:8 * p + 8, :] = jnp.where(own, 0.0, s_ref[8 * p:8 * p + 8, :]) - update[8 * p:8 * p + 8, :]

def finish_kernel(nb, g_ref, c_ref, rt_ref, t_ref, r_out, c_out, rem_out, s, v, r, blk, inv):
    n = g_ref.shape[0]
    b = n // nb
    s[...] = g_ref[...]
    rowb = lax.broadcasted_iota(jnp.int32, (n, n), 0) // b
    colb = lax.broadcasted_iota(jnp.int32, (n, n), 1) // b
    rowcol = lax.broadcasted_iota(jnp.int32, (b, n), 1)
    rowrow = lax.broadcasted_iota(jnp.int32, (b, n), 0)
    @pl.loop(0, nb)
    def _(step):
        off = pl.multiple_of(step * b, b)
        blk[...] = s[pl.ds(off, b), pl.ds(off, b)]
        factor_block(blk, inv)
        y = jnp.dot(inv[...], s[pl.ds(off, b), :], precision=HI, preferred_element_type=F32)
        r[pl.ds(off, b), :] = jnp.where(rowcol >= rowrow + off, y, 0.0)
        v[pl.ds(off, b), :] = jnp.where(rowcol < off, y, 0.0)
        v[pl.ds(off, b), pl.ds(off, b)] = inv[...]
        coef = jnp.where(rowcol >= off + b, y, 0.0)
        own = jnp.where(rowcol >= off + b, y, v[pl.ds(off, b), :])
        upd = lax.dot_general(coef, own, (((0,), (0,)), ((), ())), precision=HI, preferred_element_type=F32)
        s[...] = jnp.where((colb == step) & (rowb > step), 0.0, s[...]) - upd
    coup = jnp.dot(v[...], c_ref[...], precision=HI, preferred_element_type=F32)
    s[...] = coup
    w = lax.dot_general(v[...], coup, (((0,), (0,)), ((), ())), precision=HI, preferred_element_type=F32)
    rem_out[...] = t_ref[...] - lax.dot_general(rt_ref[...], w, (((0,), (0,)), ((), ())), precision=HI, preferred_element_type=F32)
    height = r_out.shape[0]
    pos = pl.multiple_of(lax.axis_index("frames") * height, height)
    r_out[...] = r[pl.ds(pos, height), :]
    c_out[...] = s[pl.ds(pos, height), :]

def finish(g, c, rt, t, height, nb=4):
    n, m = c.shape
    b = n // nb
    vm = pl.BlockSpec(memory_space=pltpu.VMEM)
    return pl.pallas_call(
        functools.partial(finish_kernel, nb),
        out_shape=(jax.ShapeDtypeStruct((height, n), F32), jax.ShapeDtypeStruct((height, m), F32), jax.ShapeDtypeStruct(t.shape, F32)),
        in_specs=[vm] * 4, out_specs=(vm,) * 3,
        scratch_shapes=[pltpu.VMEM((n, n), F32)] * 3 + [pltpu.VMEM((b, b), F32)] * 2,
        compiler_params=pltpu.CompilerParams(vmem_limit_bytes=48 * 2**20),
        name="finish",
    )(g, c, rt, t)


def body(dims, panel, trailing):
    frames = dims[0] * dims[1] * dims[2]
    rt, gram, cross = reduce_products(dims, panel, trailing)
    return finish(gram, cross, rt, trailing, gram.shape[0] // frames)


def solution(mesh):
    dims = (*frame_dims(mesh.shape["frames"]), mesh.shape["cols"])
    return jax.shard_map(
        functools.partial(body, dims),
        mesh=mesh,
        in_specs=(P("frames", "cols"), P("frames", "cols")),
        out_specs=(P("frames", None), P("frames", "cols"), P("frames", "cols")),
        check_vma=False,
    )
```

```python
import functools

import jax
import jax.numpy as jnp
from jax import lax
from jax.experimental import pallas as pl
from jax.experimental.pallas import tpu as pltpu
from jax.sharding import PartitionSpec as P

HI = lax.Precision.HIGHEST
F32 = jnp.float32
BLOCK = 128
MESH = pl.DeviceIdType.MESH


def frame_dims(frames):
    return {64: (4, 8, 2), 8: (2, 2, 2)}[frames]


def sum_slots(ref):
    total = ref[0]
    for slot in range(1, ref.shape[0]):
        total = total + ref[slot]
    return total


def split3(v):
    h = v.astype(jnp.bfloat16).astype(F32)
    rest = v - h
    m = rest.astype(jnp.bfloat16).astype(F32)
    low = rest - m
    return h, m, low

def lane(v, c):
    return jnp.broadcast_to(v[:, c:c + 1], v.shape)

def factor_block(s_ref, m_ref):
    n = s_ref.shape[0]
    steps = n // 8
    sub = lax.broadcasted_iota(jnp.int32, (8, n), 0)
    col = lax.broadcasted_iota(jnp.int32, (8, n), 1)
    x = [jnp.broadcast_to(s_ref[i:i + 1, :], (8, n)) for i in range(8)]
    d = [[lane(x[i], k) for k in range(i + 1)] for i in range(8)]
    for j in range(steps):
        base = 8 * j
        own = (col >= base) & (col < base + 8)
        x = [jnp.where(own, jnp.where(col == base + i, 1.0, 0.0), x[i]) for i in range(8)]
        u = []
        low = [[None] * 8 for _ in range(8)]
        for k in range(8):
            scale = lax.rsqrt(d[k][k])
            for i in range(k + 1, 8):
                low[i][k] = d[i][k] * scale
            for i in range(k + 1, 8):
                for m in range(k + 1, i + 1):
                    d[i][m] = d[i][m] - low[i][k] * low[m][k]
            u.append(x[k] * scale)
            for i in range(k + 1, 8):
                x[i] = x[i] - low[i][k] * u[k]
        packed = u[7]
        for k in range(7):
            packed = jnp.where(sub == k, u[k], packed)
        m_ref[base:base + 8, :] = jnp.where(col < base + 8, packed, 0.0)
        if j == steps - 1:
            break
        nxt = base + 8
        if j + 2 < steps:
            h, mid, lo = split3(packed)
            left = jnp.concatenate([h, h, mid, mid, h, lo], axis=0).astype(jnp.bfloat16)
            right = jnp.concatenate([h, mid, h, mid, lo, h], axis=0).astype(jnp.bfloat16)
            update = lax.dot_general(left, right, (((0,), (0,)), ((), ())), preferred_element_type=F32)
        x = [jnp.broadcast_to(s_ref[nxt + i:nxt + i + 1, :], (8, n)) for i in range(8)]
        d = [[lane(x[i], nxt + k) for k in range(i + 1)] for i in range(8)]
        x = [jnp.where(own, 0.0, v) for v in x]
        for k in range(8):
            w = [lane(u[k], nxt + i) for i in range(8)]
            for i in range(8):
                x[i] = x[i] - w[i] * u[k]
                for m in range(i + 1):
                    d[i][m] = d[i][m] - w[i] * w[m]
        if j + 2 < steps:
            for p in range(j + 2, steps):
                s_ref[8 * p:8 * p + 8, :] = jnp.where(own, 0.0, s_ref[8 * p:8 * p + 8, :]) - update[8 * p:8 * p + 8, :]


def dot3(a, b, dims):
    ah, bh = a.astype(jnp.bfloat16), b.astype(jnp.bfloat16)
    al = (a - ah.astype(F32)).astype(jnp.bfloat16)
    bl = (b - bh.astype(F32)).astype(jnp.bfloat16)

    def one(u, v):
        return lax.dot_general(u, v, (dims, ((), ())), preferred_element_type=F32)

    return one(ah, bh) + (one(ah, bl) + one(al, bh))


def factor_step(step, b, s, v, r, blk, inv):
    n = s.shape[0]
    off = pl.multiple_of(step * b, b)
    wide = pl.ds(off, b)
    rowb = lax.broadcasted_iota(jnp.int32, (n, n), 0) // b
    colb = lax.broadcasted_iota(jnp.int32, (n, n), 1) // b
    col = lax.broadcasted_iota(jnp.int32, (b, n), 1)
    row = lax.broadcasted_iota(jnp.int32, (b, n), 0)
    blk[...] = s[wide, wide]
    factor_block(blk, inv)
    y = jnp.dot(inv[...], s[wide, :], precision=HI, preferred_element_type=F32)
    r[wide, :] = jnp.where(col >= row + off, y, 0.0)
    v[wide, :] = jnp.where(col < off, y, 0.0)
    v[wide, wide] = inv[...]
    coef = jnp.where(col >= off + b, y, 0.0)
    both = jnp.where(col >= off + b, y, v[wide, :])
    upd = lax.dot_general(coef, both, (((0,), (0,)), ((), ())), precision=HI, preferred_element_type=F32)
    s[...] = jnp.where((colb == step) & (rowb > step), 0.0, s[...]) - upd


def factor_kernel(
    dims, panel_ref, trail_hbm, rt_ref, c_ref, r_ref, v_ref,
    trail, gp, gcore, gs, gx, gy, g_ref, xs, xo, xcore, xx, xr, xy, s, blk, inv,
    load_sem, ring_send, ring_recv, core_send, core_recv, x_send, x_recv, y_send, y_recv, z_send, z_recv,
):
    nx, ny, nq, nz = dims
    f = lax.axis_index("frames")
    z = lax.axis_index("cols")
    q = lax.rem(f, nq)
    y = lax.rem(f // nq, ny)
    x = f // (nq * ny)
    xto = [lax.rem(x + d, nx) for d in range(nx)]
    yto = [lax.rem(y + d, ny) for d in range(ny)]
    zto = [lax.rem(z + d, nz) for d in range(nz)]
    other = lax.rem(q + 1, nq)

    def device(x=x, y=y, q=q, z=z):
        return ((x * ny + y) * nq + q, z)

    core = device(q=other)
    xdev = [device(x=to) for to in xto]
    ydev = [device(y=to) for to in yto]
    zdev = [device(z=to) for to in zto]
    load = pltpu.make_async_copy(trail_hbm, trail, load_sem)
    load.start()
    barrier = pltpu.get_barrier_semaphore()
    partners = [core] + xdev[1:] + ydev[1:] + zdev[1:]
    for to in partners:
        pl.semaphore_signal(barrier, inc=1, device_id=to, device_id_type=MESH)
    width = panel_ref.shape[0]
    rt_ref[pl.ds(pl.multiple_of(z * width, width), width), :] = panel_ref[...]
    pl.semaphore_wait(barrier, len(partners))

    pending = []

    def link(src, dst, send, recv, to):
        return pltpu.make_async_remote_copy(
            src_ref=src, dst_ref=dst, send_sem=send, recv_sem=recv, device_id=to, device_id_type=MESH
        )

    def push(copies):
        for copy in copies:
            copy.start()
            pending.append(copy)
        return copies

    def arrived(copies):
        for copy in copies:
            copy.wait_recv()

    def drain():
        for copy in pending:
            copy.wait_send()

    def along_core(stage, src, dst):
        return [link(src, dst, core_send.at[stage], core_recv.at[stage], core)]

    def along_x(stage, src, dst):
        return [
            link(src(xto[d]), dst, x_send.at[stage, d], x_recv.at[stage, d], xdev[d]) for d in range(1, nx)
        ]

    def along_y(stage, src, dst):
        return [
            link(src(yto[d]), dst, y_send.at[stage, d], y_recv.at[stage, d], ydev[d]) for d in range(1, ny)
        ]

    half = width // 2
    last = nz // 2 - 1
    moving = {}
    for hop in range(nz // 2):
        for piece in range(2):
            for way in range(2):
                if hop == last and piece != way:
                    continue
                if hop > 0:
                    moving[hop - 1, piece, way].wait_recv()
                owner, there = (zto[-hop], zdev[1]) if way == 0 else (zto[hop], zdev[-1])
                block = rt_ref.at[pl.ds(pl.multiple_of(owner * width + piece * half, half), half), :]
                copy = link(block, block, ring_send.at[way, hop, piece], ring_recv.at[way, hop, piece], there)
                moving[hop, piece, way] = copy
                push([copy])
    for key in moving:
        if (key[0] + 1, key[1], key[2]) not in moving:
            moving[key].wait_recv()

    g_core = along_core(0, gp.at[other], gcore)
    g_x = along_x(0, lambda to: gs.at[to], gx.at[x])
    g_y = along_y(0, lambda to: gy.at[y], gy.at[y])
    mine = g_ref.at[z, q, x]
    g_z = [link(mine, mine, z_send.at[d], z_recv.at[d], zdev[d]) for d in range(1, nz)]
    g_ax = along_x(2, lambda to: g_ref.at[:, q, x], g_ref.at[:, q, x])
    g_acore = along_core(2, g_ref.at[:, q], g_ref.at[:, q])
    x_core = along_core(1, xs, xcore)
    x_x = along_x(1, lambda to: xo.at[to], xx.at[x])
    x_y = along_y(1, lambda to: xr.at[to], xy.at[y])
    x_ay = along_y(2, lambda to: c_ref.at[q, x, y], c_ref.at[q, x, y])
    x_ax = along_x(3, lambda to: c_ref.at[q, x], c_ref.at[q, x])
    x_acore = along_core(3, c_ref.at[q], c_ref.at[q])
    rows = rt_ref.shape[0] // nq

    def cross(part):
        left = rt_ref[pl.ds(pl.multiple_of(part * rows, rows), rows), :]
        return dot3(left, trail[...], ((1,), (0,))).reshape(xs.shape)

    own = rt_ref[pl.ds(pl.multiple_of(z * width, width), width), :]
    gp[...] = lax.dot_general(
        own, rt_ref[...], (((1,), (1,)), ((), ())), precision=HI, preferred_element_type=F32
    ).reshape(gp.shape)
    push(g_core)
    load.wait()
    xs[...] = cross(other)
    push(x_core)
    arrived(g_core)
    gs[...] = gp[q] + gcore[...]
    gx[x] = gs[x]
    push(g_x)
    xo[...] = cross(q)
    arrived(x_core)
    xo[...] = xo[...] + xcore[...]
    xx[x] = xo[x]
    push(x_x)
    arrived(g_x)
    gy[y] = sum_slots(gx)
    push(g_y)
    arrived(g_y)
    g_ref[z, q, x] = sum_slots(gy)
    push(g_z)
    arrived(g_z)
    push(g_ax)
    arrived(x_x)
    xr[...] = sum_slots(xx)
    xy[y] = xr[y]
    push(x_y)
    arrived(g_ax)
    push(g_acore)
    arrived(x_y)
    c_ref[q, x, y] = sum_slots(xy)
    push(x_ay)
    arrived(g_acore)
    n = s.shape[0]
    s[...] = g_ref[...].reshape(n, n)
    b = blk.shape[0]

    @pl.loop(0, n // b)
    def _(block):
        factor_step(block, b, s, v_ref, r_ref, blk, inv)

        @pl.when(block == 0)
        def _():
            arrived(x_ay)
            push(x_ax)

        @pl.when(block == 2)
        def _():
            arrived(x_ax)
            push(x_acore)
    arrived(x_acore)
    drain()


def factor(dims, panel_t, trail):
    nx, ny, nq, nz = dims
    width, height = panel_t.shape
    cols = trail.shape[1]
    n = width * nz
    rg = n // (nz * nq * nx)
    rx = n // (nq * nx * ny)
    b = BLOCK
    vm = pl.BlockSpec(memory_space=pltpu.VMEM)
    dma = pltpu.SemaphoreType.DMA
    group = pltpu.VMEM((nx, rg, n), F32)
    half = pltpu.VMEM((nx, ny, rx, cols), F32)
    rt, c, r, v = pl.pallas_call(
        functools.partial(factor_kernel, dims),
        out_shape=(
            jax.ShapeDtypeStruct((n, height), F32),
            jax.ShapeDtypeStruct((nq, nx, ny, rx, cols), F32),
            jax.ShapeDtypeStruct((n, n), F32),
            jax.ShapeDtypeStruct((n, n), F32),
        ),
        in_specs=[vm, pl.BlockSpec(memory_space=pl.ANY)],
        out_specs=(vm,) * 4,
        scratch_shapes=[
            pltpu.VMEM(trail.shape, F32),
            pltpu.VMEM((nq, nx, rg, n), F32),
            group, group, group,
            pltpu.VMEM((ny, rg, n), F32),
            pltpu.VMEM((nz, nq, nx, rg, n), F32),
            half, half, half, half,
            pltpu.VMEM((ny, rx, cols), F32),
            pltpu.VMEM((ny, rx, cols), F32),
            pltpu.VMEM((n, n), F32),
            pltpu.VMEM((b, b), F32),
            pltpu.VMEM((b, b), F32),
            dma,
            dma((2, nz // 2, 2)), dma((2, nz // 2, 2)),
            dma((4,)), dma((4,)),
            dma((4, nx)), dma((4, nx)),
            dma((3, ny)), dma((3, ny)),
            dma((nz,)), dma((nz,)),
        ],
        compiler_params=pltpu.CompilerParams(
            collective_id=0, has_side_effects=True, vmem_limit_bytes=40 * 2**20
        ),
        name="factor",
    )(panel_t, trail)
    return rt, c.reshape(n, cols), r, v


def apply_kernel(c_ref, r_ref, v_ref, rt_ref, t_ref, r_out, c_out, rem_out, coup):
    coup[...] = dot3(v_ref[...], c_ref[...], ((1,), (0,)))
    basis_t = dot3(v_ref[...], rt_ref[...], ((1,), (0,)))
    rem_out[...] = t_ref[...] - dot3(basis_t, coup[...], ((0,), (0,)))
    height = r_out.shape[0]
    pos = pl.multiple_of(lax.axis_index("frames") * height, height)
    r_out[...] = r_ref[pl.ds(pos, height), :]
    c_out[...] = coup[pl.ds(pos, height), :]


def apply(c, r, v, rt, t, height):
    n, m = c.shape
    vm = pl.BlockSpec(memory_space=pltpu.VMEM)
    return pl.pallas_call(
        apply_kernel,
        out_shape=(
            jax.ShapeDtypeStruct((height, n), F32),
            jax.ShapeDtypeStruct((height, m), F32),
            jax.ShapeDtypeStruct(t.shape, F32),
        ),
        in_specs=[vm] * 5,
        out_specs=(vm,) * 3,
        scratch_shapes=[pltpu.VMEM((n, m), F32)],
        compiler_params=pltpu.CompilerParams(vmem_limit_bytes=40 * 2**20),
        name="apply",
    )(c, r, v, rt, t)


def body(dims, panel, trailing):
    frames = dims[0] * dims[1] * dims[2]
    rt, cross, r, v = factor(dims, panel.T, trailing)
    return apply(cross, r, v, rt, trailing, r.shape[0] // frames)


def solution(mesh):
    dims = (*frame_dims(mesh.shape["frames"]), mesh.shape["cols"])
    return jax.shard_map(
        functools.partial(body, dims),
        mesh=mesh,
        in_specs=(P("frames", "cols"), P("frames", "cols")),
        out_specs=(P("frames", None), P("frames", "cols"), P("frames", "cols")),
        check_vma=False,
    )
```

```python
import functools

import jax
import jax.numpy as jnp
from jax import lax
from jax.experimental import pallas as pl
from jax.experimental.pallas import tpu as pltpu
from jax.sharding import PartitionSpec as P

HI = lax.Precision.HIGHEST
F32 = jnp.float32
BLOCK = 128
PIECES = 4
MESH = pl.DeviceIdType.MESH


def frame_dims(frames):
    return {64: (4, 8, 2), 8: (2, 2, 2)}[frames]


def sum_slots(ref):
    total = ref[0]
    for slot in range(1, ref.shape[0]):
        total = total + ref[slot]
    return total


def split3(v):
    h = v.astype(jnp.bfloat16).astype(F32)
    rest = v - h
    m = rest.astype(jnp.bfloat16).astype(F32)
    low = rest - m
    return h, m, low

def lane(v, c):
    return jnp.broadcast_to(v[:, c:c + 1], v.shape)

def factor_block(s_ref, m_ref):
    n = s_ref.shape[0]
    steps = n // 8
    sub = lax.broadcasted_iota(jnp.int32, (8, n), 0)
    col = lax.broadcasted_iota(jnp.int32, (8, n), 1)
    x = [jnp.broadcast_to(s_ref[i:i + 1, :], (8, n)) for i in range(8)]
    d = [[lane(x[i], k) for k in range(i + 1)] for i in range(8)]
    for j in range(steps):
        base = 8 * j
        own = (col >= base) & (col < base + 8)
        x = [jnp.where(own, jnp.where(col == base + i, 1.0, 0.0), x[i]) for i in range(8)]
        u = []
        low = [[None] * 8 for _ in range(8)]
        for k in range(8):
            scale = lax.rsqrt(d[k][k])
            for i in range(k + 1, 8):
                low[i][k] = d[i][k] * scale
            for i in range(k + 1, 8):
                for m in range(k + 1, i + 1):
                    d[i][m] = d[i][m] - low[i][k] * low[m][k]
            u.append(x[k] * scale)
            for i in range(k + 1, 8):
                x[i] = x[i] - low[i][k] * u[k]
        packed = u[7]
        for k in range(7):
            packed = jnp.where(sub == k, u[k], packed)
        m_ref[base:base + 8, :] = jnp.where(col < base + 8, packed, 0.0)
        if j == steps - 1:
            break
        nxt = base + 8
        if j + 2 < steps:
            h, mid, lo = split3(packed)
            left = jnp.concatenate([h, h, mid, mid, h, lo], axis=0).astype(jnp.bfloat16)
            right = jnp.concatenate([h, mid, h, mid, lo, h], axis=0).astype(jnp.bfloat16)
            update = lax.dot_general(left, right, (((0,), (0,)), ((), ())), preferred_element_type=F32)
        x = [jnp.where(own, 0.0, jnp.broadcast_to(s_ref[nxt + i:nxt + i + 1, :], (8, n))) for i in range(8)]
        for k in range(8):
            for i in range(8):
                x[i] = x[i] - lane(u[k], nxt + i) * u[k]
        d = [[lane(x[i], nxt + m) for m in range(i + 1)] for i in range(8)]
        if j + 2 < steps:
            for p in range(j + 2, steps):
                s_ref[8 * p:8 * p + 8, :] = jnp.where(own, 0.0, s_ref[8 * p:8 * p + 8, :]) - update[8 * p:8 * p + 8, :]


def dot3(a, b, dims):
    ah, bh = a.astype(jnp.bfloat16), b.astype(jnp.bfloat16)
    al = (a - ah.astype(F32)).astype(jnp.bfloat16)
    bl = (b - bh.astype(F32)).astype(jnp.bfloat16)

    def one(u, v):
        return lax.dot_general(u, v, (dims, ((), ())), preferred_element_type=F32)

    return one(ah, bh) + (one(ah, bl) + one(al, bh))


def factor_step(step, b, s, v, r, blk, inv):
    n = s.shape[0]
    off = pl.multiple_of(step * b, b)
    wide = pl.ds(off, b)
    rowb = lax.broadcasted_iota(jnp.int32, (n, n), 0) // b
    colb = lax.broadcasted_iota(jnp.int32, (n, n), 1) // b
    col = lax.broadcasted_iota(jnp.int32, (b, n), 1)
    row = lax.broadcasted_iota(jnp.int32, (b, n), 0)
    blk[...] = s[wide, wide]
    factor_block(blk, inv)
    y = jnp.dot(inv[...], s[wide, :], precision=HI, preferred_element_type=F32)
    r[wide, :] = jnp.where(col >= row + off, y, 0.0)
    v[wide, :] = jnp.where(col < off, y, 0.0)
    v[wide, wide] = inv[...]

    @pl.when(off + b < n)
    def _():
        coef = jnp.where(col >= off + b, y, 0.0)
        both = jnp.where(col >= off + b, y, v[wide, :])
        upd = lax.dot_general(coef, both, (((0,), (0,)), ((), ())), precision=HI, preferred_element_type=F32)
        s[...] = jnp.where((colb == step) & (rowb > step), 0.0, s[...]) - upd


def factor_kernel(
    dims, panel_hbm, trail_hbm, rt_ref, c_ref, r_ref, v_ref, trail,
    gp, gcore, gs, gx, gy, g_ref, xs, xo, xcore, xx, xr, xy, s, blk, inv,
    load_sem, ring_send, ring_recv, core_send, core_recv, x_send, x_recv, y_send, y_recv, z_send, z_recv,
    gx_send, gx_recv, gc_send, gc_recv,
):
    nx, ny, nq, nz = dims
    f = lax.axis_index("frames")
    z = lax.axis_index("cols")
    q = lax.rem(f, nq)
    y = lax.rem(f // nq, ny)
    x = f // (nq * ny)
    xto = [lax.rem(x + d, nx) for d in range(nx)]
    yto = [lax.rem(y + d, ny) for d in range(ny)]
    zto = [lax.rem(z + d, nz) for d in range(nz)]
    other = lax.rem(q + 1, nq)

    def device(x=x, y=y, q=q, z=z):
        return ((x * ny + y) * nq + q, z)

    core = device(q=other)
    xdev = [device(x=to) for to in xto]
    ydev = [device(y=to) for to in yto]
    zdev = [device(z=to) for to in zto]
    width = panel_hbm.shape[0]
    mine = rt_ref.at[pl.ds(pl.multiple_of(z * width, width), width), :]
    fetch = pltpu.make_async_copy(panel_hbm, mine, load_sem.at[0])
    fetch.start()
    load = pltpu.make_async_copy(trail_hbm, trail, load_sem.at[1])
    load.start()
    barrier = pltpu.get_barrier_semaphore()
    partners = [core] + xdev[1:] + ydev[1:] + zdev[1:]
    for to in partners:
        pl.semaphore_signal(barrier, inc=1, device_id=to, device_id_type=MESH)
    fetch.wait()
    pl.semaphore_wait(barrier, len(partners))

    pending = []

    def link(src, dst, send, recv, to):
        return pltpu.make_async_remote_copy(
            src_ref=src, dst_ref=dst, send_sem=send, recv_sem=recv, device_id=to, device_id_type=MESH
        )

    def push(copies):
        for copy in copies:
            copy.start()
            pending.append(copy)
        return copies

    def arrived(copies):
        for copy in copies:
            copy.wait_recv()

    def drain():
        for copy in pending:
            copy.wait_send()

    def along_core(stage, src, dst):
        return [link(src, dst, core_send.at[stage], core_recv.at[stage], core)]

    def along_x(stage, src, dst):
        return [
            link(src(xto[d]), dst, x_send.at[stage, d], x_recv.at[stage, d], xdev[d]) for d in range(1, nx)
        ]

    def along_y(stage, src, dst):
        return [
            link(src(yto[d]), dst, y_send.at[stage, d], y_recv.at[stage, d], ydev[d]) for d in range(1, ny)
        ]

    part = width // PIECES
    last = nz // 2 - 1
    moving = {}
    for hop in range(nz // 2):
        for piece in range(PIECES):
            for way in range(2):
                if hop == last and piece % 2 != way:
                    continue
                if hop > 0:
                    moving[hop - 1, piece, way].wait_recv()
                owner, there = (zto[-hop], zdev[1]) if way == 0 else (zto[hop], zdev[-1])
                block = rt_ref.at[pl.ds(pl.multiple_of(owner * width + piece * part, part), part), :]
                copy = link(block, block, ring_send.at[way, hop, piece], ring_recv.at[way, hop, piece], there)
                moving[hop, piece, way] = copy
                push([copy])
    for key in moving:
        if (key[0] + 1, key[1], key[2]) not in moving:
            moving[key].wait_recv()

    g_core = along_core(0, gp.at[other], gcore)
    g_x = along_x(0, lambda to: gs.at[to], gx.at[x])
    g_y = along_y(0, lambda to: gy.at[y], gy.at[y])
    near_z = sorted(range(nz), key=lambda d: min(d, nz - d))
    near_x = sorted(range(1, nx), key=lambda d: min(d, nx - d))
    rows_g = {(dz, dx): g_ref.at[zto[-dz], q, xto[-dx]] for dz in range(nz) for dx in range(nx)}
    g_z = {d: link(rows_g[0, 0], rows_g[0, 0], z_send.at[d], z_recv.at[d], zdev[d]) for d in range(1, nz)}
    g_ax = {
        (dz, dx): link(rows_g[dz, 0], rows_g[dz, 0], gx_send.at[dz, dx], gx_recv.at[dz, dx], xdev[dx])
        for dz in range(nz)
        for dx in range(1, nx)
    }
    g_ac = {
        key: link(rows_g[key], rows_g[key], gc_send.at[key], gc_recv.at[key], core) for key in rows_g
    }
    x_core = along_core(1, xs, xcore)
    x_x = along_x(1, lambda to: xo.at[to], xx.at[x])
    x_y = along_y(1, lambda to: xr.at[to], xy.at[y])
    x_ay = along_y(2, lambda to: c_ref.at[q, x, y], c_ref.at[q, x, y])
    x_ax = along_x(3, lambda to: c_ref.at[q, x], c_ref.at[q, x])
    x_acore = along_core(3, c_ref.at[q], c_ref.at[q])
    rows = rt_ref.shape[0] // nq

    def cross(part):
        left = rt_ref[pl.ds(pl.multiple_of(part * rows, rows), rows), :]
        return dot3(left, trail[...], ((1,), (0,))).reshape(xs.shape)

    own = rt_ref[pl.ds(pl.multiple_of(z * width, width), width), :]
    gp[...] = lax.dot_general(
        own, rt_ref[...], (((1,), (1,)), ((), ())), precision=HI, preferred_element_type=F32
    ).reshape(gp.shape)
    push(g_core)
    load.wait()
    xs[...] = cross(other)
    push(x_core)
    arrived(g_core)
    gs[...] = gp[q] + gcore[...]
    gx[x] = gs[x]
    push(g_x)
    xo[...] = cross(q)
    arrived(x_core)
    xo[...] = xo[...] + xcore[...]
    xx[x] = xo[x]
    push(x_x)
    arrived(g_x)
    gy[y] = sum_slots(gx)
    push(g_y)
    arrived(g_y)
    g_ref[z, q, x] = sum_slots(gy)
    push([g_z[d] for d in reversed(near_z[1:])])
    for dz in near_z:
        if dz > 0:
            arrived([g_z[dz]])
        push([g_ax[dz, dx] for dx in near_x])
        push([g_ac[dz, 0]])
    arrived(x_x)
    xr[...] = sum_slots(xx)
    xy[y] = xr[y]
    push(x_y)
    for dz in near_z:
        for dx in near_x:
            arrived([g_ax[dz, dx]])
            push([g_ac[dz, dx]])
    arrived(x_y)
    c_ref[q, x, y] = sum_slots(xy)
    push(x_ay)
    arrived(g_ac.values())
    n = s.shape[0]
    s[...] = g_ref[...].reshape(n, n)
    b = blk.shape[0]

    @pl.loop(0, n // b)
    def _(block):
        factor_step(block, b, s, v_ref, r_ref, blk, inv)

        @pl.when(block == 0)
        def _():
            arrived(x_ay)
            push(x_ax)

        @pl.when(block == 2)
        def _():
            arrived(x_ax)
            push(x_acore)
    arrived(x_acore)
    drain()


def in_hbm(array):
    return pltpu.with_memory_space_constraint(array, pltpu.HBM)


def factor(dims, panel_t, trail):
    nx, ny, nq, nz = dims
    width, height = panel_t.shape
    cols = trail.shape[1]
    n = width * nz
    rg = n // (nz * nq * nx)
    rx = n // (nq * nx * ny)
    b = BLOCK
    vm = pl.BlockSpec(memory_space=pltpu.VMEM)
    dma = pltpu.SemaphoreType.DMA
    group = pltpu.VMEM((nx, rg, n), F32)
    half = pltpu.VMEM((nx, ny, rx, cols), F32)
    rt, c, r, v, t = pl.pallas_call(
        functools.partial(factor_kernel, dims),
        out_shape=(
            jax.ShapeDtypeStruct((n, height), F32),
            jax.ShapeDtypeStruct((nq, nx, ny, rx, cols), F32),
            jax.ShapeDtypeStruct((n, n), F32),
            jax.ShapeDtypeStruct((n, n), F32),
            jax.ShapeDtypeStruct(trail.shape, F32),
        ),
        in_specs=[pl.BlockSpec(memory_space=pltpu.HBM)] * 2,
        out_specs=(vm,) * 5,
        scratch_shapes=[
            pltpu.VMEM((nq, nx, rg, n), F32),
            group, group, group,
            pltpu.VMEM((ny, rg, n), F32),
            pltpu.VMEM((nz, nq, nx, rg, n), F32),
            half, half, half, half,
            pltpu.VMEM((ny, rx, cols), F32),
            pltpu.VMEM((ny, rx, cols), F32),
            pltpu.VMEM((n, n), F32),
            pltpu.VMEM((b, b), F32),
            pltpu.VMEM((b, b), F32),
            dma((2,)),
            dma((2, nz // 2, PIECES)), dma((2, nz // 2, PIECES)),
            dma((4,)), dma((4,)),
            dma((4, nx)), dma((4, nx)),
            dma((3, ny)), dma((3, ny)),
            dma((nz,)), dma((nz,)),
            dma((nz, nx)), dma((nz, nx)),
            dma((nz, nx)), dma((nz, nx)),
        ],
        compiler_params=pltpu.CompilerParams(
            collective_id=0, has_side_effects=True, vmem_limit_bytes=40 * 2**20
        ),
        name="factor",
    )(in_hbm(panel_t), in_hbm(trail))
    return rt, c.reshape(n, cols), r, v, t


def apply_kernel(c_ref, r_ref, v_ref, rt_ref, t_ref, r_out, c_out, rem_out, coup):
    coup[...] = dot3(v_ref[...], c_ref[...], ((1,), (0,)))
    basis_t = dot3(v_ref[...], rt_ref[...], ((1,), (0,)))
    rem_out[...] = t_ref[...] - dot3(basis_t, coup[...], ((0,), (0,)))
    height = r_out.shape[0]
    pos = pl.multiple_of(lax.axis_index("frames") * height, height)
    r_out[...] = r_ref[pl.ds(pos, height), :]
    c_out[...] = coup[pl.ds(pos, height), :]


def apply(c, r, v, rt, t, height):
    n, m = c.shape
    vm = pl.BlockSpec(memory_space=pltpu.VMEM)
    return pl.pallas_call(
        apply_kernel,
        out_shape=(
            jax.ShapeDtypeStruct((height, n), F32),
            jax.ShapeDtypeStruct((height, m), F32),
            jax.ShapeDtypeStruct(t.shape, F32),
        ),
        in_specs=[vm] * 5,
        out_specs=(vm,) * 3,
        scratch_shapes=[pltpu.VMEM((n, m), F32)],
        compiler_params=pltpu.CompilerParams(vmem_limit_bytes=40 * 2**20),
        name="apply",
    )(c, r, v, rt, t)


def body(dims, panel, trailing):
    frames = dims[0] * dims[1] * dims[2]
    rt, cross, r, v, t = factor(dims, panel.T, trailing)
    return apply(cross, r, v, rt, t, r.shape[0] // frames)


def solution(mesh):
    dims = (*frame_dims(mesh.shape["frames"]), mesh.shape["cols"])
    return jax.shard_map(
        functools.partial(body, dims),
        mesh=mesh,
        in_specs=(P("frames", "cols"), P("frames", "cols")),
        out_specs=(P("frames", None), P("frames", "cols"), P("frames", "cols")),
        check_vma=False,
    )
```

```python
import functools

import jax
import jax.numpy as jnp
from jax import lax
from jax.experimental import pallas as pl
from jax.experimental.pallas import tpu as pltpu
from jax.sharding import PartitionSpec as P

HI = lax.Precision.HIGHEST
F32 = jnp.float32
BLOCK = 128
PIECES = 4
MESH = pl.DeviceIdType.MESH


def frame_dims(frames):
    return {64: (4, 8, 2), 8: (2, 2, 2)}[frames]


def sum_slots(ref):
    total = ref[0]
    for slot in range(1, ref.shape[0]):
        total = total + ref[slot]
    return total


def split3(v):
    h = v.astype(jnp.bfloat16).astype(F32)
    rest = v - h
    m = rest.astype(jnp.bfloat16).astype(F32)
    low = rest - m
    return h, m, low

def lane(v, c):
    return jnp.broadcast_to(v[:, c:c + 1], v.shape)

EARLY = 0
GROUPS = ((0, 1, 2, 3), (4, 5), (6,), (7,))


def factor_block(s_ref, m_ref, w_ref):
    n = s_ref.shape[0]
    steps = n // 8
    sub = lax.broadcasted_iota(jnp.int32, (8, n), 0)
    col = lax.broadcasted_iota(jnp.int32, (8, n), 1)
    x = [jnp.broadcast_to(s_ref[i:i + 1, :], (8, n)) for i in range(8)]
    d = [[lane(x[i], k) for k in range(i + 1)] for i in range(8)]
    for j in range(steps):
        base = 8 * j
        own = (col >= base) & (col < base + 8)
        x = [jnp.where(own, jnp.where(col == base + i, 1.0, 0.0), x[i]) for i in range(8)]
        u = []
        low = [[None] * 8 for _ in range(8)]
        for k in range(8):
            scale = lax.rsqrt(d[k][k])
            for i in range(k + 1, 8):
                low[i][k] = d[i][k] * scale
            for i in range(k + 1, 8):
                for m in range(k + 1, i + 1):
                    d[i][m] = d[i][m] - low[i][k] * low[m][k]
            u.append(x[k] * scale)
            for i in range(k + 1, 8):
                x[i] = x[i] - low[i][k] * u[k]
        packed = u[7]
        for k in range(7):
            packed = jnp.where(sub == k, u[k], packed)
        m_ref[base:base + 8, :] = jnp.where(col < base + 8, packed, 0.0)
        if j == steps - 1:
            break
        nxt = base + 8
        if j + 3 < steps:
            h, mid, lo = split3(packed)
            left = jnp.concatenate([h, h, mid, mid, h, lo], axis=0).astype(jnp.bfloat16)
            right = jnp.concatenate([h, mid, h, mid, lo, h], axis=0).astype(jnp.bfloat16)
            update = lax.dot_general(left, right, (((0,), (0,)), ((), ())), preferred_element_type=F32)

        def below(rows_at, y, groups, first, early=0):
            for slot, group in enumerate(groups, first):
                if len(group) == 1:
                    w = {(group[0], i): lane(u[group[0]], rows_at + i) for i in range(8)}
                else:
                    some = u[group[-1]]
                    for k in group[:-1]:
                        some = jnp.where(sub == k, u[k], some)
                    for i in range(8):
                        w_ref[j % 2, slot, i] = lane(some, rows_at + i)
                    w = {
                        (k, i): jnp.broadcast_to(w_ref[j % 2, slot, i, k:k + 1, :], (8, n))
                        for k in group
                        for i in range(8)
                    }
                for k in group:
                    for i in range(8):
                        y[i] = y[i] - w[k, i] * u[k]
                        for m in range(min(early, i + 1)):
                            d[i][m] = d[i][m] - w[k, i] * w[k, m]
            return y

        def rows_of(at):
            return [jnp.broadcast_to(s_ref[at + i:at + i + 1, :], (8, n)) for i in range(8)]

        x = ahead if j > 0 else rows_of(nxt)
        d = [[lane(x[i], nxt + m) if m < EARLY else None for m in range(i + 1)] for i in range(8)]
        x = [jnp.where(own, 0.0, v) for v in x]
        x = below(nxt, x, GROUPS, 0, EARLY)
        for i in range(8):
            for m in range(EARLY, i + 1):
                d[i][m] = lane(x[i], nxt + m)
        if j + 2 < steps:
            ahead = [jnp.where(own, 0.0, v) for v in rows_of(nxt + 8)]
            ahead = below(nxt + 8, ahead, (tuple(range(8)),), len(GROUPS))
        if j + 3 < steps:
            for p in range(j + 3, steps):
                s_ref[8 * p:8 * p + 8, :] = jnp.where(own, 0.0, s_ref[8 * p:8 * p + 8, :]) - update[8 * p:8 * p + 8, :]


def dot3(a, b, dims):
    ah, bh = a.astype(jnp.bfloat16), b.astype(jnp.bfloat16)
    al = (a - ah.astype(F32)).astype(jnp.bfloat16)
    bl = (b - bh.astype(F32)).astype(jnp.bfloat16)

    def one(u, v):
        return lax.dot_general(u, v, (dims, ((), ())), preferred_element_type=F32)

    return one(ah, bh) + (one(ah, bl) + one(al, bh))


def factor_step(step, b, s, v, r, blk, inv, wide_ref):
    n = s.shape[0]
    off = step * b
    end = off + b
    blk[...] = s[off:end, off:end]
    factor_block(blk, inv, wide_ref)
    y = jnp.dot(inv[...], s[off:end, :], precision=HI, preferred_element_type=F32)
    col = lax.broadcasted_iota(jnp.int32, (b, b), 1)
    row = lax.broadcasted_iota(jnp.int32, (b, b), 0)
    r[off:end, off:end] = jnp.where(col >= row, y[:, off:end], 0.0)
    v[off:end, off:end] = inv[...]
    if off > 0:
        r[off:end, :off] = jnp.zeros((b, off), F32)
        v[off:end, :off] = y[:, :off]
    if end < n:
        right = y[:, end:]
        r[off:end, end:] = right
        v[off:end, end:] = jnp.zeros((b, n - end), F32)

        def take(lo, hi, coef, part, fresh):
            upd = lax.dot_general(coef, part, (((0,), (0,)), ((), ())), precision=HI, preferred_element_type=F32)
            s[end:, lo:hi] = -upd if fresh else s[end:, lo:hi] - upd

        take(end, n, right, right, False)
        take(off, end, right, inv[...], True)
        if off > 0:
            take(0, off, right, y[:, :off], False)


def far_first(n):
    return sorted(range(1, n), key=lambda d: -min(d, n - d))


def factor_kernel(
    dims, panel_hbm, trail_hbm, rt_ref, c_ref, r_ref, v_ref, trail,
    gp, gcore, gs, gx, gy, g_ref, xs, xo, xcore, xx, xr, xy, s, blk, inv, wide,
    load_sem, ring_send, ring_recv, core_send, core_recv, x_send, x_recv, y_send, y_recv, z_send, z_recv,
    gx_send, gx_recv, gc_send, gc_recv,
):
    nx, ny, nq, nz = dims
    f = lax.axis_index("frames")
    z = lax.axis_index("cols")
    q = lax.rem(f, nq)
    y = lax.rem(f // nq, ny)
    x = f // (nq * ny)
    xto = [lax.rem(x + d, nx) for d in range(nx)]
    yto = [lax.rem(y + d, ny) for d in range(ny)]
    zto = [lax.rem(z + d, nz) for d in range(nz)]
    other = lax.rem(q + 1, nq)

    def device(x=x, y=y, q=q, z=z):
        return ((x * ny + y) * nq + q, z)

    core = device(q=other)
    xdev = [device(x=to) for to in xto]
    ydev = [device(y=to) for to in yto]
    zdev = [device(z=to) for to in zto]
    width = panel_hbm.shape[0]
    mine = rt_ref.at[pl.ds(pl.multiple_of(z * width, width), width), :]
    fetch = pltpu.make_async_copy(panel_hbm, mine, load_sem.at[0])
    fetch.start()
    load = pltpu.make_async_copy(trail_hbm, trail, load_sem.at[1])
    load.start()
    barrier = pltpu.get_barrier_semaphore()
    partners = [core] + xdev[1:] + ydev[1:] + zdev[1:]
    for to in partners:
        pl.semaphore_signal(barrier, inc=1, device_id=to, device_id_type=MESH)
    fetch.wait()
    pl.semaphore_wait(barrier, len(partners))

    pending = []

    def link(src, dst, send, recv, to):
        return pltpu.make_async_remote_copy(
            src_ref=src, dst_ref=dst, send_sem=send, recv_sem=recv, device_id=to, device_id_type=MESH
        )

    def push(copies):
        for copy in copies:
            copy.start()
            pending.append(copy)
        return copies

    def arrived(copies):
        for copy in copies:
            copy.wait_recv()

    def drain():
        for copy in pending:
            copy.wait_send()

    def along_core(stage, src, dst):
        return [link(src, dst, core_send.at[stage], core_recv.at[stage], core)]

    def along_x(stage, src, dst):
        return [
            link(src(xto[d]), dst, x_send.at[stage, d], x_recv.at[stage, d], xdev[d]) for d in far_first(nx)
        ]

    def along_y(stage, src, dst):
        return [
            link(src(yto[d]), dst, y_send.at[stage, d], y_recv.at[stage, d], ydev[d]) for d in far_first(ny)
        ]

    part = width // PIECES
    last = nz // 2 - 1
    moving = {}
    for hop in range(nz // 2):
        for piece in range(PIECES):
            for way in range(2):
                if hop == last and piece % 2 != way:
                    continue
                if hop > 0:
                    moving[hop - 1, piece, way].wait_recv()
                owner, there = (zto[-hop], zdev[1]) if way == 0 else (zto[hop], zdev[-1])
                block = rt_ref.at[pl.ds(pl.multiple_of(owner * width + piece * part, part), part), :]
                copy = link(block, block, ring_send.at[way, hop, piece], ring_recv.at[way, hop, piece], there)
                moving[hop, piece, way] = copy
                push([copy])
    for key in moving:
        if (key[0] + 1, key[1], key[2]) not in moving:
            moving[key].wait_recv()

    g_core = along_core(0, gp.at[other], gcore)
    g_x = along_x(0, lambda to: gs.at[to], gx.at[x])
    g_y = along_y(0, lambda to: gy.at[y], gy.at[y])
    near_z = sorted(range(nz), key=lambda d: min(d, nz - d))
    near_x = sorted(range(1, nx), key=lambda d: min(d, nx - d))
    rows_g = {(dz, dx): g_ref.at[zto[-dz], q, xto[-dx]] for dz in range(nz) for dx in range(nx)}
    g_z = {d: link(rows_g[0, 0], rows_g[0, 0], z_send.at[d], z_recv.at[d], zdev[d]) for d in range(1, nz)}
    g_ax = {
        (dz, dx): link(rows_g[dz, 0], rows_g[dz, 0], gx_send.at[dz, dx], gx_recv.at[dz, dx], xdev[dx])
        for dz in range(nz)
        for dx in range(1, nx)
    }
    g_ac = {
        key: link(rows_g[key], rows_g[key], gc_send.at[key], gc_recv.at[key], core) for key in rows_g
    }
    x_core = along_core(1, xs, xcore)
    x_x = along_x(1, lambda to: xo.at[to], xx.at[x])
    x_y = along_y(1, lambda to: xr.at[to], xy.at[y])
    x_ay = along_y(2, lambda to: c_ref.at[q, x, y], c_ref.at[q, x, y])
    x_ax = along_x(3, lambda to: c_ref.at[q, x], c_ref.at[q, x])
    x_acore = along_core(3, c_ref.at[q], c_ref.at[q])
    rows = rt_ref.shape[0] // nq

    def cross(part):
        left = rt_ref[pl.ds(pl.multiple_of(part * rows, rows), rows), :]
        return dot3(left, trail[...], ((1,), (0,))).reshape(xs.shape)

    own = rt_ref[pl.ds(pl.multiple_of(z * width, width), width), :]
    gp[...] = lax.dot_general(
        own, rt_ref[...], (((1,), (1,)), ((), ())), precision=HI, preferred_element_type=F32
    ).reshape(gp.shape)
    push(g_core)
    load.wait()
    xs[...] = cross(other)
    push(x_core)
    arrived(g_core)
    gs[...] = gp[q] + gcore[...]
    gx[x] = gs[x]
    push(g_x)
    xo[...] = cross(q)
    arrived(x_core)
    xo[...] = xo[...] + xcore[...]
    xx[x] = xo[x]
    push(x_x)
    arrived(g_x)
    gy[y] = sum_slots(gx)
    push(g_y)
    arrived(g_y)
    g_ref[z, q, x] = sum_slots(gy)
    push([g_z[d] for d in far_first(nz)])
    for dz in near_z:
        if dz > 0:
            arrived([g_z[dz]])
        push([g_ax[dz, dx] for dx in near_x])
        push([g_ac[dz, 0]])
    arrived(x_x)
    xr[...] = sum_slots(xx)
    xy[y] = xr[y]
    push(x_y)
    for dz in near_z:
        for dx in near_x:
            arrived([g_ax[dz, dx]])
            push([g_ac[dz, dx]])
    arrived(x_y)
    c_ref[q, x, y] = sum_slots(xy)
    push(x_ay)
    arrived(g_ac.values())
    n = s.shape[0]
    s[...] = g_ref[...].reshape(n, n)
    b = blk.shape[0]

    for block in range(n // b):
        factor_step(block, b, s, v_ref, r_ref, blk, inv, wide)
        if block == 0:
            arrived(x_ay)
            push(x_ax)
        if block == n // b - 2:
            arrived(x_ax)
            push(x_acore)
    arrived(x_acore)
    drain()


def in_hbm(array):
    return pltpu.with_memory_space_constraint(array, pltpu.HBM)


def factor(dims, panel_t, trail):
    nx, ny, nq, nz = dims
    width, height = panel_t.shape
    cols = trail.shape[1]
    n = width * nz
    rg = n // (nz * nq * nx)
    rx = n // (nq * nx * ny)
    b = BLOCK
    vm = pl.BlockSpec(memory_space=pltpu.VMEM)
    dma = pltpu.SemaphoreType.DMA
    group = pltpu.VMEM((nx, rg, n), F32)
    half = pltpu.VMEM((nx, ny, rx, cols), F32)
    rt, c, r, v, t = pl.pallas_call(
        functools.partial(factor_kernel, dims),
        out_shape=(
            jax.ShapeDtypeStruct((n, height), F32),
            jax.ShapeDtypeStruct((nq, nx, ny, rx, cols), F32),
            jax.ShapeDtypeStruct((n, n), F32),
            jax.ShapeDtypeStruct((n, n), F32),
            jax.ShapeDtypeStruct(trail.shape, F32),
        ),
        in_specs=[pl.BlockSpec(memory_space=pltpu.HBM)] * 2,
        out_specs=(vm,) * 5,
        scratch_shapes=[
            pltpu.VMEM((nq, nx, rg, n), F32),
            group, group, group,
            pltpu.VMEM((ny, rg, n), F32),
            pltpu.VMEM((nz, nq, nx, rg, n), F32),
            half, half, half, half,
            pltpu.VMEM((ny, rx, cols), F32),
            pltpu.VMEM((ny, rx, cols), F32),
            pltpu.VMEM((n, n), F32),
            pltpu.VMEM((b, b), F32),
            pltpu.VMEM((b, b), F32),
            pltpu.VMEM((2, 8, 8, 8, b), F32),
            dma((2,)),
            dma((2, nz // 2, PIECES)), dma((2, nz // 2, PIECES)),
            dma((4,)), dma((4,)),
            dma((4, nx)), dma((4, nx)),
            dma((3, ny)), dma((3, ny)),
            dma((nz,)), dma((nz,)),
            dma((nz, nx)), dma((nz, nx)),
            dma((nz, nx)), dma((nz, nx)),
        ],
        compiler_params=pltpu.CompilerParams(
            collective_id=0, has_side_effects=True, vmem_limit_bytes=40 * 2**20
        ),
        name="factor",
    )(in_hbm(panel_t), in_hbm(trail))
    return rt, c.reshape(n, cols), r, v, t


def apply_kernel(c_ref, r_ref, v_ref, rt_ref, t_ref, r_out, c_out, rem_out, coup):
    coup[...] = dot3(v_ref[...], c_ref[...], ((1,), (0,)))
    basis_t = dot3(v_ref[...], rt_ref[...], ((1,), (0,)))
    rem_out[...] = t_ref[...] - dot3(basis_t, coup[...], ((0,), (0,)))
    height = r_out.shape[0]
    pos = pl.multiple_of(lax.axis_index("frames") * height, height)
    r_out[...] = r_ref[pl.ds(pos, height), :]
    c_out[...] = coup[pl.ds(pos, height), :]


def apply(c, r, v, rt, t, height):
    n, m = c.shape
    vm = pl.BlockSpec(memory_space=pltpu.VMEM)
    return pl.pallas_call(
        apply_kernel,
        out_shape=(
            jax.ShapeDtypeStruct((height, n), F32),
            jax.ShapeDtypeStruct((height, m), F32),
            jax.ShapeDtypeStruct(t.shape, F32),
        ),
        in_specs=[vm] * 5,
        out_specs=(vm,) * 3,
        scratch_shapes=[pltpu.VMEM((n, m), F32)],
        compiler_params=pltpu.CompilerParams(vmem_limit_bytes=40 * 2**20),
        name="apply",
    )(c, r, v, rt, t)


def body(dims, panel, trailing):
    frames = dims[0] * dims[1] * dims[2]
    rt, cross, r, v, t = factor(dims, panel.T, trailing)
    return apply(cross, r, v, rt, t, r.shape[0] // frames)


def solution(mesh):
    dims = (*frame_dims(mesh.shape["frames"]), mesh.shape["cols"])
    return jax.shard_map(
        functools.partial(body, dims),
        mesh=mesh,
        in_specs=(P("frames", "cols"), P("frames", "cols")),
        out_specs=(P("frames", None), P("frames", "cols"), P("frames", "cols")),
        check_vma=False,
    )
```

```python
import functools

import jax
import jax.numpy as jnp
from jax import lax
from jax.experimental import pallas as pl
from jax.experimental.pallas import tpu as pltpu
from jax.sharding import PartitionSpec as P

HI = lax.Precision.HIGHEST
F32 = jnp.float32
BLOCK = 128
PIECES = 4
MESH = pl.DeviceIdType.MESH


def frame_dims(frames):
    return {64: (4, 8, 2), 8: (2, 2, 2)}[frames]


def sum_slots(ref):
    total = ref[0]
    for slot in range(1, ref.shape[0]):
        total = total + ref[slot]
    return total


def split3(v):
    h = v.astype(jnp.bfloat16).astype(F32)
    rest = v - h
    m = rest.astype(jnp.bfloat16).astype(F32)
    low = rest - m
    return h, m, low

def lane(v, c):
    return jnp.broadcast_to(v[:, c:c + 1], v.shape)

EARLY = 0
GROUPS = ((0, 1, 2, 3), (4, 5), (6,), (7,))


def factor_block(s_ref, m_ref, w_ref):
    n = s_ref.shape[0]
    steps = n // 8
    sub = lax.broadcasted_iota(jnp.int32, (8, n), 0)
    col = lax.broadcasted_iota(jnp.int32, (8, n), 1)
    x = [jnp.broadcast_to(s_ref[i:i + 1, :], (8, n)) for i in range(8)]
    d = [[lane(x[i], k) for k in range(i + 1)] for i in range(8)]
    for j in range(steps):
        base = 8 * j
        own = (col >= base) & (col < base + 8)
        x = [jnp.where(own, jnp.where(col == base + i, 1.0, 0.0), x[i]) for i in range(8)]
        u = []
        low = [[None] * 8 for _ in range(8)]
        for k in range(8):
            scale = lax.rsqrt(d[k][k])
            for i in range(k + 1, 8):
                low[i][k] = d[i][k] * scale
            for i in range(k + 1, 8):
                for m in range(k + 1, i + 1):
                    d[i][m] = d[i][m] - low[i][k] * low[m][k]
            u.append(x[k] * scale)
            for i in range(k + 1, 8):
                x[i] = x[i] - low[i][k] * u[k]
        packed = u[7]
        for k in range(7):
            packed = jnp.where(sub == k, u[k], packed)
        m_ref[base:base + 8, :] = jnp.where(col < base + 8, packed, 0.0)
        if j == steps - 1:
            break
        nxt = base + 8
        if j + 3 < steps:
            h, mid, lo = split3(packed)
            left = jnp.concatenate([h, h, mid, mid, h, lo], axis=0).astype(jnp.bfloat16)
            right = jnp.concatenate([h, mid, h, mid, lo, h], axis=0).astype(jnp.bfloat16)
            update = lax.dot_general(left, right, (((0,), (0,)), ((), ())), preferred_element_type=F32)

        def below(rows_at, y, groups, first, early=0):
            for slot, group in enumerate(groups, first):
                if len(group) == 1:
                    w = {(group[0], i): lane(u[group[0]], rows_at + i) for i in range(8)}
                else:
                    some = u[group[-1]]
                    for k in group[:-1]:
                        some = jnp.where(sub == k, u[k], some)
                    for i in range(8):
                        w_ref[j % 2, slot, i] = lane(some, rows_at + i)
                    w = {
                        (k, i): jnp.broadcast_to(w_ref[j % 2, slot, i, k:k + 1, :], (8, n))
                        for k in group
                        for i in range(8)
                    }
                for k in group:
                    for i in range(8):
                        y[i] = y[i] - w[k, i] * u[k]
                        for m in range(min(early, i + 1)):
                            d[i][m] = d[i][m] - w[k, i] * w[k, m]
            return y

        def rows_of(at):
            return [jnp.broadcast_to(s_ref[at + i:at + i + 1, :], (8, n)) for i in range(8)]

        x = ahead if j > 0 else rows_of(nxt)
        d = [[lane(x[i], nxt + m) if m < EARLY else None for m in range(i + 1)] for i in range(8)]
        x = [jnp.where(own, 0.0, v) for v in x]
        x = below(nxt, x, GROUPS, 0, EARLY)
        for i in range(8):
            for m in range(EARLY, i + 1):
                d[i][m] = lane(x[i], nxt + m)
        if j + 2 < steps:
            ahead = [jnp.where(own, 0.0, v) for v in rows_of(nxt + 8)]
            ahead = below(nxt + 8, ahead, (tuple(range(8)),), len(GROUPS))
        if j + 3 < steps:
            for p in range(j + 3, steps):
                s_ref[8 * p:8 * p + 8, :] = jnp.where(own, 0.0, s_ref[8 * p:8 * p + 8, :]) - update[8 * p:8 * p + 8, :]


def dot3(a, b, dims):
    ah, bh = a.astype(jnp.bfloat16), b.astype(jnp.bfloat16)
    al = (a - ah.astype(F32)).astype(jnp.bfloat16)
    bl = (b - bh.astype(F32)).astype(jnp.bfloat16)

    def one(u, v):
        return lax.dot_general(u, v, (dims, ((), ())), preferred_element_type=F32)

    return one(ah, bh) + (one(ah, bl) + one(al, bh))


def factor_step(step, b, s, v, r, blk, inv, wide_ref):
    n = s.shape[0]
    off = step * b
    end = off + b
    if off > 0:
        blk[...] = s[off:end, off:end]
        factor_block(blk, inv, wide_ref)
    y = jnp.dot(inv[...], s[off:end, :], precision=HI, preferred_element_type=F32)
    col = lax.broadcasted_iota(jnp.int32, (b, b), 1)
    row = lax.broadcasted_iota(jnp.int32, (b, b), 0)
    r[off:end, off:end] = jnp.where(col >= row, y[:, off:end], 0.0)
    v[off:end, off:end] = inv[...]
    if off > 0:
        r[off:end, :off] = jnp.zeros((b, off), F32)
        v[off:end, :off] = y[:, :off]
    if end < n:
        right = y[:, end:]
        r[off:end, end:] = right
        v[off:end, end:] = jnp.zeros((b, n - end), F32)

        def take(lo, hi, coef, part, fresh):
            upd = lax.dot_general(coef, part, (((0,), (0,)), ((), ())), precision=HI, preferred_element_type=F32)
            s[end:, lo:hi] = -upd if fresh else s[end:, lo:hi] - upd

        take(end, n, right, right, False)
        take(off, end, right, inv[...], True)
        if off > 0:
            take(0, off, right, y[:, :off], False)


def far_first(n):
    return sorted(range(1, n), key=lambda d: -min(d, n - d))


def factor_kernel(
    dims, panel_hbm, trail_hbm, rt_ref, c_ref, r_ref, v_ref, trail,
    gp, gcore, gs, gx, gy, g_ref, xs, xo, xcore, xx, xr, xy, s, blk, inv, wide,
    load_sem, ring_send, ring_recv, core_send, core_recv, x_send, x_recv, y_send, y_recv, z_send, z_recv,
    gx_send, gx_recv, gc_send, gc_recv,
):
    nx, ny, nq, nz = dims
    f = lax.axis_index("frames")
    z = lax.axis_index("cols")
    q = lax.rem(f, nq)
    y = lax.rem(f // nq, ny)
    x = f // (nq * ny)
    xto = [lax.rem(x + d, nx) for d in range(nx)]
    yto = [lax.rem(y + d, ny) for d in range(ny)]
    zto = [lax.rem(z + d, nz) for d in range(nz)]
    other = lax.rem(q + 1, nq)

    def device(x=x, y=y, q=q, z=z):
        return ((x * ny + y) * nq + q, z)

    core = device(q=other)
    xdev = [device(x=to) for to in xto]
    ydev = [device(y=to) for to in yto]
    zdev = [device(z=to) for to in zto]
    width = panel_hbm.shape[0]
    mine = rt_ref.at[pl.ds(pl.multiple_of(z * width, width), width), :]
    fetch = pltpu.make_async_copy(panel_hbm, mine, load_sem.at[0])
    fetch.start()
    load = pltpu.make_async_copy(trail_hbm, trail, load_sem.at[1])
    load.start()
    barrier = pltpu.get_barrier_semaphore()
    partners = [core] + xdev[1:] + ydev[1:] + zdev[1:]
    for to in partners:
        pl.semaphore_signal(barrier, inc=1, device_id=to, device_id_type=MESH)
    fetch.wait()
    pl.semaphore_wait(barrier, len(partners))

    pending = []

    def link(src, dst, send, recv, to):
        return pltpu.make_async_remote_copy(
            src_ref=src, dst_ref=dst, send_sem=send, recv_sem=recv, device_id=to, device_id_type=MESH
        )

    def push(copies):
        for copy in copies:
            copy.start()
            pending.append(copy)
        return copies

    def arrived(copies):
        for copy in copies:
            copy.wait_recv()

    def drain():
        for copy in pending:
            copy.wait_send()

    def along_core(stage, src, dst):
        return [link(src, dst, core_send.at[stage], core_recv.at[stage], core)]

    def along_x(stage, src, dst):
        return [
            link(src(xto[d]), dst, x_send.at[stage, d], x_recv.at[stage, d], xdev[d]) for d in far_first(nx)
        ]

    def along_y(stage, src, dst):
        return [
            link(src(yto[d]), dst, y_send.at[stage, d], y_recv.at[stage, d], ydev[d]) for d in far_first(ny)
        ]

    part = width // PIECES
    last = nz // 2 - 1
    moving = {}
    for hop in range(nz // 2):
        for piece in range(PIECES):
            for way in range(2):
                if hop == last and piece % 2 != way:
                    continue
                if hop > 0:
                    moving[hop - 1, piece, way].wait_recv()
                owner, there = (zto[-hop], zdev[1]) if way == 0 else (zto[hop], zdev[-1])
                block = rt_ref.at[pl.ds(pl.multiple_of(owner * width + piece * part, part), part), :]
                copy = link(block, block, ring_send.at[way, hop, piece], ring_recv.at[way, hop, piece], there)
                moving[hop, piece, way] = copy
                push([copy])
    for key in moving:
        if (key[0] + 1, key[1], key[2]) not in moving:
            moving[key].wait_recv()

    g_core = along_core(0, gp.at[other], gcore)
    g_x = along_x(0, lambda to: gs.at[to], gx.at[x])
    g_y = along_y(0, lambda to: gy.at[y], gy.at[y])
    near_x = sorted(range(1, nx), key=lambda d: min(d, nx - d))
    rows_g = {(dz, dx): g_ref.at[dz, q, xto[-dx]] for dz in range(nz) for dx in range(nx)}
    mine = g_ref.at[z, q, x]
    g_z = [link(mine, mine, z_send.at[d], z_recv.at[z], zdev[d]) for d in far_first(nz)]
    from_z = [link(rows_g[at, 0], rows_g[at, 0], z_send.at[0], z_recv.at[at], core) for at in range(nz)]
    g_ax = {
        (dz, dx): link(rows_g[dz, 0], rows_g[dz, 0], gx_send.at[dz, dx], gx_recv.at[dz, dx], xdev[dx])
        for dz in range(nz)
        for dx in range(1, nx)
    }
    g_ac = {
        key: link(rows_g[key], rows_g[key], gc_send.at[key], gc_recv.at[key], core) for key in rows_g
    }
    x_core = along_core(1, xs, xcore)
    x_x = along_x(1, lambda to: xo.at[to], xx.at[x])
    x_y = along_y(1, lambda to: xr.at[to], xy.at[y])
    x_ay = along_y(2, lambda to: c_ref.at[q, x, y], c_ref.at[q, x, y])
    x_ax = along_x(3, lambda to: c_ref.at[q, x], c_ref.at[q, x])
    x_acore = along_core(3, c_ref.at[q], c_ref.at[q])
    rows = rt_ref.shape[0] // nq

    def cross(part):
        left = rt_ref[pl.ds(pl.multiple_of(part * rows, rows), rows), :]
        return dot3(left, trail[...], ((1,), (0,))).reshape(xs.shape)

    own = rt_ref[pl.ds(pl.multiple_of(z * width, width), width), :]
    gp[...] = lax.dot_general(
        own, rt_ref[...], (((1,), (1,)), ((), ())), precision=HI, preferred_element_type=F32
    ).reshape(gp.shape)
    push(g_core)
    load.wait()
    xs[...] = cross(other)
    push(x_core)
    arrived(g_core)
    gs[...] = gp[q] + gcore[...]
    gx[x] = gs[x]
    push(g_x)
    xo[...] = cross(q)
    arrived(x_core)
    xo[...] = xo[...] + xcore[...]
    xx[x] = xo[x]
    push(x_x)
    arrived(g_x)
    gy[y] = sum_slots(gx)
    push(g_y)
    arrived(g_y)
    g_ref[z, q, x] = sum_slots(gy)
    push(g_z)
    for dz in range(nz):

        @pl.when(z != dz)
        def _():
            from_z[dz].wait_recv()

        push([g_ax[dz, dx] for dx in near_x])
        push([g_ac[dz, 0]])
    arrived(x_x)
    xr[...] = sum_slots(xx)
    xy[y] = xr[y]
    push(x_y)
    for dz in range(nz):
        for dx in near_x:
            arrived([g_ax[dz, dx]])
            push([g_ac[dz, dx]])
    arrived(x_y)
    c_ref[q, x, y] = sum_slots(xy)
    push(x_ay)
    n = s.shape[0]
    b = blk.shape[0]
    early = nz * b // n
    arrived([g_ac[key] for key in g_ac if key[0] < early])
    s[:b, :] = g_ref[:early].reshape(b, n)
    blk[...] = s[:b, :b]
    factor_block(blk, inv, wide)
    arrived([g_ac[key] for key in g_ac if key[0] >= early])
    s[b:, :] = g_ref[early:].reshape(n - b, n)

    for block in range(n // b):
        factor_step(block, b, s, v_ref, r_ref, blk, inv, wide)
        if block == 0:
            arrived(x_ay)
            push(x_ax)
        if block == n // b - 2:
            arrived(x_ax)
            push(x_acore)
    arrived(x_acore)
    drain()


def in_hbm(array):
    return pltpu.with_memory_space_constraint(array, pltpu.HBM)


def factor(dims, panel_t, trail):
    nx, ny, nq, nz = dims
    width, height = panel_t.shape
    cols = trail.shape[1]
    n = width * nz
    rg = n // (nz * nq * nx)
    rx = n // (nq * nx * ny)
    b = BLOCK
    vm = pl.BlockSpec(memory_space=pltpu.VMEM)
    dma = pltpu.SemaphoreType.DMA
    group = pltpu.VMEM((nx, rg, n), F32)
    half = pltpu.VMEM((nx, ny, rx, cols), F32)
    rt, c, r, v, t = pl.pallas_call(
        functools.partial(factor_kernel, dims),
        out_shape=(
            jax.ShapeDtypeStruct((n, height), F32),
            jax.ShapeDtypeStruct((nq, nx, ny, rx, cols), F32),
            jax.ShapeDtypeStruct((n, n), F32),
            jax.ShapeDtypeStruct((n, n), F32),
            jax.ShapeDtypeStruct(trail.shape, F32),
        ),
        in_specs=[pl.BlockSpec(memory_space=pltpu.HBM)] * 2,
        out_specs=(vm,) * 5,
        scratch_shapes=[
            pltpu.VMEM((nq, nx, rg, n), F32),
            group, group, group,
            pltpu.VMEM((ny, rg, n), F32),
            pltpu.VMEM((nz, nq, nx, rg, n), F32),
            half, half, half, half,
            pltpu.VMEM((ny, rx, cols), F32),
            pltpu.VMEM((ny, rx, cols), F32),
            pltpu.VMEM((n, n), F32),
            pltpu.VMEM((b, b), F32),
            pltpu.VMEM((b, b), F32),
            pltpu.VMEM((2, 8, 8, 8, b), F32),
            dma((2,)),
            dma((2, nz // 2, PIECES)), dma((2, nz // 2, PIECES)),
            dma((4,)), dma((4,)),
            dma((4, nx)), dma((4, nx)),
            dma((3, ny)), dma((3, ny)),
            dma((nz,)), dma((nz,)),
            dma((nz, nx)), dma((nz, nx)),
            dma((nz, nx)), dma((nz, nx)),
        ],
        compiler_params=pltpu.CompilerParams(
            collective_id=0, has_side_effects=True, vmem_limit_bytes=40 * 2**20
        ),
        name="factor",
    )(in_hbm(panel_t), in_hbm(trail))
    return rt, c.reshape(n, cols), r, v, t


def apply_kernel(c_ref, r_ref, v_ref, rt_ref, t_ref, r_out, c_out, rem_out, coup):
    coup[...] = dot3(v_ref[...], c_ref[...], ((1,), (0,)))
    basis_t = dot3(v_ref[...], rt_ref[...], ((1,), (0,)))
    rem_out[...] = t_ref[...] - dot3(basis_t, coup[...], ((0,), (0,)))
    height = r_out.shape[0]
    pos = pl.multiple_of(lax.axis_index("frames") * height, height)
    r_out[...] = r_ref[pl.ds(pos, height), :]
    c_out[...] = coup[pl.ds(pos, height), :]


def apply(c, r, v, rt, t, height):
    n, m = c.shape
    vm = pl.BlockSpec(memory_space=pltpu.VMEM)
    return pl.pallas_call(
        apply_kernel,
        out_shape=(
            jax.ShapeDtypeStruct((height, n), F32),
            jax.ShapeDtypeStruct((height, m), F32),
            jax.ShapeDtypeStruct(t.shape, F32),
        ),
        in_specs=[vm] * 5,
        out_specs=(vm,) * 3,
        scratch_shapes=[pltpu.VMEM((n, m), F32)],
        compiler_params=pltpu.CompilerParams(vmem_limit_bytes=40 * 2**20),
        name="apply",
    )(c, r, v, rt, t)


def body(dims, panel, trailing):
    frames = dims[0] * dims[1] * dims[2]
    rt, cross, r, v, t = factor(dims, panel.T, trailing)
    return apply(cross, r, v, rt, t, r.shape[0] // frames)


def solution(mesh):
    dims = (*frame_dims(mesh.shape["frames"]), mesh.shape["cols"])
    return jax.shard_map(
        functools.partial(body, dims),
        mesh=mesh,
        in_specs=(P("frames", "cols"), P("frames", "cols")),
        out_specs=(P("frames", None), P("frames", "cols"), P("frames", "cols")),
        check_vma=False,
    )
```
